32 devices in a mesh: row: 8 (over z, core), col: 4 (over y, x).
Axes of the slice: x: 2, y: 2, z: 4, core: 2. Of those that a mesh axis runs over, the one named last changes fastest.
Arguments:
- labels_prior: float32 [16, 65536], P(None, ('row', 'col')), may hold values from 0.05 to 1
- tiles: bfloat16 [7168, 128, 128], P(('row', 'col')), may hold values from 0 to 1
- tile_rows: int32 [7168], P(('row', 'col')), may hold values from 0 to 63, as said below
- tile_cols: int32 [7168], P(('row', 'col')), may hold values from 0 to 127, as said below
- tile_count: int32 [32], P(('row', 'col')), may hold values from 28 to 224, as said below
Outputs:
- scores: float32 [16, 65536], P(None, ('row', 'col'))
The draws below stay inside these ranges and needn't reach their ends.
Inputs may be any that keep to these rules, and one draw needn't show every extreme that they name: `tile_rows`: block rows within a row group of 16 * 4 blocks; both ends occur. `tile_cols`: block columns within a column group of 16 * 8 blocks; both ends occur. `tile_count`: loads are skewed; some device uses all 224 slots.
All inputs are finite; a program needn't handle non-finite values.
Results may differ from the reference program's by a relative error of at most 0.0003.
Values may be sent and summed in bfloat16 or wider, within the bound.
A program may use at most 64 MiB of HBM per device.

```python
import math
import jax
import jax.numpy as jnp
from jax import lax

TILE = 128
LABELS = 16
BPP = 16
ITERS = 2
CAP = 224
NODES = 65536
N_ROW = 8
N_COL = 4


def draw_tile_rows(key, part):
    total = N_ROW * N_COL * CAP
    inner = jax.random.fold_in(key, 11)
    values = jax.random.randint(inner, (total,), 0, N_COL * BPP, dtype=jnp.int32)
    return values.at[0].set(0).at[total - 1].set(N_COL * BPP - 1)


def draw_tile_cols(key, part):
    total = N_ROW * N_COL * CAP
    inner = jax.random.fold_in(key, 12)
    values = jax.random.randint(inner, (total,), 0, N_ROW * BPP, dtype=jnp.int32)
    return values.at[1].set(N_ROW * BPP - 1).at[total - 2].set(0)


def draw_tile_count(key, part):
    devices = N_ROW * N_COL
    lowest = CAP // 8
    inner = jax.random.fold_in(key, 13)
    first = jax.random.randint(jax.random.fold_in(inner, 1), (devices,), 0, CAP - lowest + 1, dtype=jnp.int32)
    second = jax.random.randint(jax.random.fold_in(inner, 2), (devices,), 0, CAP - lowest + 1, dtype=jnp.int32)
    counts = lowest + jnp.minimum(first, second)
    busiest = jax.random.randint(jax.random.fold_in(inner, 3), (), 0, devices, dtype=jnp.int32)
    return jnp.where(jnp.arange(devices, dtype=jnp.int32) == busiest, CAP, counts).astype(jnp.int32)


def shard_levels(own_key, shape, split, least, top_value):
    def one(axis_at, blocks):
        steps = jax.random.uniform(jax.random.fold_in(jax.random.fold_in(own_key, 6), axis_at), (blocks,), jnp.float32, least / len(split), top_value / len(split))
        return jnp.repeat(jnp.exp(steps), shape[axis_at] // blocks).reshape((-1,) + (1,) * (len(shape) - axis_at - 1))

    gain = one(*split[0])
    for cut in split[1:]:
        gain = gain * one(*cut)
    return gain


def setup_inputs(seed: int = 0) -> dict:
    streams_of = jax.random.split(jax.random.key(seed), 6)
    labels_prior = jnp.clip(jnp.exp(math.log(1.0) - 2.9957323 * jax.random.uniform(streams_of[0], (LABELS, NODES), jnp.float32) ** shard_levels(streams_of[0], (LABELS, NODES), ((1, 32),), -0.2, 0.2)), 0.05, 1.0)
    tiles = jnp.clip(1.0 * jax.random.uniform(streams_of[1], (N_ROW * N_COL * CAP, TILE, TILE), jnp.float32) ** shard_levels(streams_of[1], (N_ROW * N_COL * CAP, TILE, TILE), ((0, 32),), -0.2, 0.2), 0.0, 1.0).astype(jnp.bfloat16)
    tile_rows = draw_tile_rows(jax.random.fold_in(streams_of[5], 71), 0)
    tile_cols = draw_tile_cols(jax.random.fold_in(streams_of[5], 71), 0)
    tile_count = draw_tile_count(jax.random.fold_in(streams_of[5], 71), 0)
    return dict(labels_prior=labels_prior, tiles=tiles, tile_rows=tile_rows, tile_cols=tile_cols, tile_count=tile_count)


spread_weight = 0.9


def reference(labels_prior, tiles, tile_rows, tile_cols, tile_count):
    devices = N_ROW * N_COL
    group_blocks = N_COL * BPP
    group_nodes = group_blocks * TILE
    tile_four = tiles.reshape(devices, CAP, TILE, TILE)
    rows_two = tile_rows.reshape(devices, CAP)
    cols_two = tile_cols.reshape(devices, CAP)
    slot_ids = jnp.arange(CAP, dtype=jnp.int32)
    block_ids = jnp.arange(group_blocks, dtype=jnp.int32)
    device_ids = jnp.arange(devices, dtype=jnp.int32)

    def hot_rows(device):
        valid = (slot_ids < tile_count[device]).astype(jnp.float32)
        return (rows_two[device][:, None] == block_ids[None, :]).astype(jnp.float32) * valid[:, None]

    def global_cols(device):
        column = device % N_COL
        local = cols_two[device]
        return ((local // BPP * N_COL + column) * BPP + local % BPP).astype(jnp.int32)

    def degree_step(total, device):
        rowsum = jnp.sum(tile_four[device].astype(jnp.float32), axis=2)
        part = jnp.einsum("sr,si->ri", hot_rows(device), rowsum, precision=lax.Precision.HIGHEST).reshape(-1)
        start = ((device // N_COL) * group_nodes).astype(jnp.int32)
        current = lax.dynamic_slice_in_dim(total, start, group_nodes, 0)
        return lax.dynamic_update_slice_in_dim(total, current + part, start, 0), None

    degree = lax.scan(degree_step, jnp.zeros((NODES,), jnp.float32), device_ids)[0] + 1.0

    scores = labels_prior
    for step in range(ITERS):
        blocks = scores.astype(jnp.bfloat16).reshape(LABELS, NODES // TILE, TILE)

        def add_device(total, device):
            picked = jnp.take(blocks, global_cols(device), axis=1)
            terms = jnp.einsum("lsj,sij->sli", picked.astype(jnp.float32), tile_four[device].astype(jnp.float32), precision=lax.Precision.HIGHEST)
            part = jnp.einsum("sr,sli->lri", hot_rows(device), terms, precision=lax.Precision.HIGHEST).reshape(LABELS, group_nodes)
            start = ((device // N_COL) * group_nodes).astype(jnp.int32)
            current = lax.dynamic_slice_in_dim(total, start, group_nodes, 1)
            return lax.dynamic_update_slice_in_dim(total, current + part, start, 1), None

        sums = lax.scan(add_device, jnp.zeros((LABELS, NODES), jnp.float32), device_ids)[0]
        scores = spread_weight * (sums + scores) / degree[None, :] + (1.0 - spread_weight) * labels_prior
    return scores
```

```python
import functools

import jax
import jax.numpy as jnp
from jax import lax
from jax.experimental import pallas as pl
from jax.experimental.pallas import tpu as pltpu
from jax.sharding import PartitionSpec as P

ITERS = 2
SPREAD = 0.9
LEVELS = 65535.0
GROUPS = 2
LOADS = 7


def plan(rows, cols, count, table_ref, keep_ref, group_blocks):
    slots = rows.shape[1]
    lane = lax.broadcasted_iota(jnp.int32, (slots, slots), 1)
    down = lax.broadcasted_iota(jnp.int32, (slots, slots), 0)
    row = jnp.where(lane[0:1] < count, rows, group_blocks)
    key = row * slots + lane[0:1]
    same = lane == down

    def stand(x):
        return jnp.sum(jnp.where(same, x, 0), axis=1, keepdims=True)

    key_down, row_down, col_down = stand(key), stand(row), stand(cols)
    rank = jnp.sum((key < key_down).astype(jnp.int32), axis=1, keepdims=True)
    hit = rank == lane

    def lie(cond, x):
        return jnp.sum(jnp.where(cond, x, 0), axis=0, keepdims=True)

    here = lie(hit, row_down + 1)
    before = lie(rank + 1 == lane, row_down + 1)
    table_ref[0:1, 0:slots] = lie(hit, down)
    table_ref[1:2, 0:slots] = lie(hit, col_down)
    keep = stand((here == before).astype(jnp.int32)).astype(jnp.float32)
    keep_ref[...] = jnp.broadcast_to(keep, keep_ref.shape)
    group = lax.broadcasted_iota(jnp.int32, (slots, group_blocks), 1)
    stop = jnp.sum((row_down <= group).astype(jnp.int32), axis=0, keepdims=True)
    start = jnp.sum((row_down < group).astype(jnp.int32), axis=0, keepdims=True)
    table_ref[2:3, 0:group_blocks] = jnp.maximum(stop - 1, 0)
    table_ref[3:4, 0:group_blocks] = (stop > start).astype(jnp.int32)
    block = lax.broadcasted_iota(jnp.int32, (group_blocks, slots), 0)
    return (block == row).astype(jnp.float32)


def kernel(
    n_row, n_col,
    prior_hbm, tiles_hbm, slot_rows_ref, slot_cols_ref, count_ref,
    out_ref,
    prior_ref, tiles_ref, ag_ref, upper_ref, lower_ref, run_ref, rows_ref, inv_ref, rows_in_ref, code_ref, code_in_ref,
    cur_ref, scale_ref, table_ref, plan_ref, keep_ref, slot_sum_ref,
    prior_sem, load_sem, plan_sem, ag_send, ag_recv, rs_send, rs_recv, row_send, row_recv,
):
    labels, piece = prior_ref.shape
    slots, tile, _ = tiles_ref.shape
    own = piece // tile
    pairs = own // 2
    some = labels // GROUPS
    n_z = n_row // 2
    my_row = lax.axis_index("row")
    my_col = lax.axis_index("col")
    my_z = my_row // 2
    my_core = my_row % 2
    partner = my_z * 2 + (1 - my_core)

    def at(row, col):
        return {"row": row, "col": col}

    def part(g):
        return pl.ds(g * some, some)

    prior_copies = []
    for g in range(GROUPS):
        prior_copies.append(
            pltpu.make_async_copy(prior_hbm.at[part(g)], prior_ref.at[part(g)], prior_sem.at[g])
        )
        prior_copies[-1].start()

    barrier = pltpu.get_barrier_semaphore()
    z_to = [None] + [((my_z + d) % n_z) * 2 + my_core for d in range(1, n_z)]
    z_from = [None] + [((my_z + n_z - d) % n_z) * 2 + my_core for d in range(1, n_z)]
    p_from = [partner] + [((my_z + n_z - d) % n_z) * 2 + (1 - my_core) for d in range(1, n_z)]
    c_to = [None] + [(my_col + d) % n_col for d in range(1, n_col)]
    c_from = [None] + [(my_col + n_col - d) % n_col for d in range(1, n_col)]
    for d in range(1, n_z):
        pl.semaphore_signal(barrier, inc=1, device_id=at(z_to[d], my_col))
    pl.semaphore_signal(barrier, inc=1, device_id=at(partner, my_col))
    for d in range(1, n_col):
        pl.semaphore_signal(barrier, inc=1, device_id=at(my_row, c_to[d]))

    loads = []
    step = slots // LOADS
    for n in range(LOADS):
        window = pl.ds(n * step, step)
        loads.append(
            pltpu.make_async_copy(tiles_hbm.at[window], tiles_ref.at[window], load_sem.at[n])
        )
        loads[-1].start()

    sent = []

    def gather_copy(it, g, src_row, slot, to_row):
        window = pl.ds(src_row * pairs, pairs)
        return pltpu.make_async_remote_copy(
            src_ref=ag_ref.at[it, g, window],
            dst_ref=ag_ref.at[it, g, window],
            send_sem=ag_send.at[it, g, slot],
            recv_sem=ag_recv.at[it, g, slot],
            device_id=at(to_row, my_col),
        )

    def expand(it, g, src_row):
        def one(t, carry):
            both = ag_ref[it, g, src_row * pairs + t].astype(jnp.float32)
            blank = jnp.zeros((some, tile), jnp.float32)
            b = src_row * own + 2 * t
            for i, half in enumerate((both[:some], both[some:])):
                upper_ref[b + i] = jnp.concatenate([half, blank], axis=0).astype(jnp.bfloat16)
                lower_ref[b + i] = jnp.concatenate([blank, half], axis=0).astype(jnp.bfloat16)
            return carry

        lax.fori_loop(0, pairs, one, 0, unroll=True)

    def gather_start(it, g):
        copies = [gather_copy(it, g, my_row, d, z_to[d]) for d in range(1, n_z)]
        copies.append(gather_copy(it, g, my_row, n_z, partner))
        for copy in copies:
            copy.start()
        sent.extend(copies)

    def gather_finish(it, g):
        expand(it, g, my_row)
        for d in range(1, n_z):
            gather_copy(it, g, z_from[d], d, z_to[d]).wait_recv()
            copy = gather_copy(it, g, z_from[d], n_z + d, partner)
            copy.start()
            sent.append(copy)
        for d in range(1, n_z):
            expand(it, g, z_from[d])
        for d in range(n_z):
            gather_copy(it, g, p_from[d], n_z + d, partner).wait_recv()
            expand(it, g, p_from[d])

    def lanes(b):
        return pl.ds(pl.multiple_of(b * tile, tile), tile)

    for g in range(GROUPS):

        def round_prior(t, carry):
            both = [prior_ref[part(g), lanes(2 * t + i)] for i in range(2)]
            ag_ref[0, g, my_row * pairs + t] = jnp.concatenate(both, axis=0).astype(jnp.bfloat16)
            return carry

        prior_copies[g].wait()
        lax.fori_loop(0, pairs, round_prior, 0, unroll=True)
        if g == 0:
            pl.semaphore_wait(barrier, n_z + n_col - 1)
        gather_start(0, g)

    def product(left, right):
        return lax.dot_general(
            left, right, (((1,), (0,)), ((), ())), preferred_element_type=jnp.float32
        )

    hot = plan(slot_rows_ref[...], slot_cols_ref[...], count_ref[0], table_ref, keep_ref, n_col * own)
    plan_copy = pltpu.make_async_copy(table_ref, plan_ref, plan_sem)
    plan_copy.start()

    def weights(slot_pair):
        return jnp.concatenate([tiles_ref[n] for n in slot_pair], axis=0)

    down = lax.broadcasted_iota(jnp.int32, (2 * some, 2 * tile), 0)
    lane = lax.broadcasted_iota(jnp.int32, (2 * some, 2 * tile), 1)
    ones = ((down < some) == (lane < tile)).astype(jnp.float32).astype(jnp.bfloat16)
    for n, copy in enumerate(loads):
        copy.wait()

        def sum_pair(m, carry):
            k = n * step + 2 * m
            for turned in (k, k + 1):
                tiles_ref[turned] = tiles_ref[turned].T
            both = product(ones, weights((k, k + 1)))
            for i in range(2):
                slot_sum_ref[pl.ds(k + i, 1), :] = both[i * some : i * some + 1]
            return carry

        lax.fori_loop(0, step // 2, sum_pair, 0, unroll=True)
    rows_ref[...] = jnp.dot(
        hot, slot_sum_ref[...], precision=lax.Precision.HIGHEST, preferred_element_type=jnp.float32
    )

    def row_copy(d):
        return pltpu.make_async_remote_copy(
            src_ref=rows_ref.at[pl.ds(pl.multiple_of(c_to[d] * own, own), own)],
            dst_ref=rows_in_ref.at[d],
            send_sem=row_send.at[d],
            recv_sem=row_recv.at[d],
            device_id=at(my_row, c_to[d]),
        )

    for d in range(1, n_col):
        copy = row_copy(d)
        copy.start()
        sent.append(copy)
    whole = rows_ref[...]
    inv_ref[...] = jnp.where(whole > 0.0, LEVELS / jnp.where(whole > 0.0, whole, 1.0), 0.0)
    plan_copy.wait()

    def code_copy(it, g, d):
        return pltpu.make_async_remote_copy(
            src_ref=code_ref.at[it, g, pl.ds(c_to[d] * pairs, pairs)],
            dst_ref=code_in_ref.at[it, g, d],
            send_sem=rs_send.at[it, g, d],
            recv_sem=rs_recv.at[it, g, d],
            device_id=at(my_row, c_to[d]),
        )

    def multiply(it, g):
        def add_pair(m, total):
            ks = (2 * m, 2 * m + 1)
            left = jnp.concatenate(
                [upper_ref[plan_ref[1, ks[0]]], lower_ref[plan_ref[1, ks[1]]]], axis=1
            )
            both = product(left, weights([plan_ref[0, k] for k in ks]))
            for i, k in enumerate(ks):
                keep = jnp.broadcast_to(keep_ref[pl.ds(k, 1), :], (some, tile))
                total = total * keep + both[i * some : (i + 1) * some]
                run_ref[g, k] = total
            return total

        lax.fori_loop(0, slots // 2, add_pair, jnp.zeros((some, tile), jnp.float32), unroll=True)

    def send_codes(it, g):
        for d in range(1, n_col):

            def encode(t, carry):
                levels = []
                for i in range(2):
                    r = c_to[d] * own + 2 * t + i
                    value = run_ref[g, plan_ref[2, r]]
                    levels.append(jnp.minimum(value * inv_ref[pl.ds(r, 1), :] + 0.5, LEVELS))
                level = jnp.concatenate(levels, axis=0).astype(jnp.int32) - 32768
                code_ref[it, g, c_to[d] * pairs + t] = level.astype(jnp.int16)
                return carry

            lax.fori_loop(0, pairs, encode, 0, unroll=True)
            copy = code_copy(it, g, d)
            copy.start()
            sent.append(copy)

    def update(it, g):
        for d in range(1, n_col):
            code_copy(it, g, d).wait_recv()

        def one(t, carry):
            found = [
                code_in_ref[it, g, d, t].astype(jnp.int32).astype(jnp.float32) + 32768.0
                for d in range(1, n_col)
            ]
            values = []
            for i in range(2):
                b = 2 * t + i
                r = my_col * own + b
                prior = prior_ref[part(g), lanes(b)]
                total = prior if it == 0 else cur_ref[g, b]
                total = total + run_ref[g, plan_ref[2, r]] * plan_ref[3, r].astype(jnp.float32)
                for d in range(1, n_col):
                    level = found[d - 1][i * some : (i + 1) * some]
                    total = total + level * (rows_in_ref[d, pl.ds(b, 1), :] * (1.0 / LEVELS))
                value = total * scale_ref[pl.ds(b, 1), :] + (1.0 - SPREAD) * prior
                if it + 1 < ITERS:
                    cur_ref[g, b] = value
                    values.append(value)
                else:
                    out_ref[part(g), lanes(b)] = value
            if it + 1 < ITERS:
                ag_ref[it + 1, g, my_row * pairs + t] = jnp.concatenate(values, axis=0).astype(jnp.bfloat16)
            return carry

        lax.fori_loop(0, pairs, one, 0, unroll=True)

    for it in range(ITERS):
        for g in range(GROUPS):
            gather_finish(it, g)
            multiply(it, g)
            send_codes(it, g)
        if it == 0:
            degree = 1.0 + rows_ref[pl.ds(pl.multiple_of(my_col * own, own), own), :]
            for d in range(1, n_col):
                row_copy(d).wait_recv()
                degree = degree + rows_in_ref[d]
            scale_ref[...] = SPREAD / degree
        for g in range(GROUPS):
            update(it, g)
            if it + 1 < ITERS:
                gather_start(it + 1, g)

    for copy in sent:
        copy.wait_send()


def local(n_row, n_col, labels_prior, tiles, tile_rows, tile_cols, tile_count):
    labels, piece = labels_prior.shape
    slots, tile, _ = tiles.shape
    own = piece // tile
    pairs = own // 2
    some = labels // GROUPS
    n_z = n_row // 2
    group = n_col * own
    smem = pl.BlockSpec(memory_space=pltpu.SMEM)
    width = -(-max(slots, group) // 128) * 128
    vmem = pl.BlockSpec(memory_space=pltpu.VMEM)
    return pl.pallas_call(
        functools.partial(kernel, n_row, n_col),
        out_shape=pltpu.VMEM((labels, piece), jnp.float32),
        in_specs=[pl.BlockSpec(memory_space=pl.ANY)] * 2 + [vmem, vmem, smem],
        out_specs=vmem,
        scratch_shapes=[
            pltpu.VMEM((labels, piece), jnp.float32),
            pltpu.VMEM((slots, tile, tile), jnp.bfloat16),
            pltpu.VMEM((ITERS, GROUPS, n_row * pairs, 2 * some, tile), jnp.bfloat16),
            pltpu.VMEM((n_row * own, 2 * some, tile), jnp.bfloat16),
            pltpu.VMEM((n_row * own, 2 * some, tile), jnp.bfloat16),
            pltpu.VMEM((GROUPS, slots, some, tile), jnp.float32),
            pltpu.VMEM((group, tile), jnp.float32),
            pltpu.VMEM((group, tile), jnp.float32),
            pltpu.VMEM((n_col, own, tile), jnp.float32),
            pltpu.VMEM((ITERS, GROUPS, n_col * pairs, 2 * some, tile), jnp.int16),
            pltpu.VMEM((ITERS, GROUPS, n_col, pairs, 2 * some, tile), jnp.int16),
            pltpu.VMEM((GROUPS, own, some, tile), jnp.float32),
            pltpu.VMEM((own, tile), jnp.float32),
            pltpu.VMEM((8, width), jnp.int32),
            pltpu.SMEM((8, width), jnp.int32),
            pltpu.VMEM((slots, tile), jnp.float32),
            pltpu.VMEM((slots, tile), jnp.float32),
            pltpu.SemaphoreType.DMA((GROUPS,)),
            pltpu.SemaphoreType.DMA((LOADS,)),
            pltpu.SemaphoreType.DMA(()),
            pltpu.SemaphoreType.DMA((ITERS, GROUPS, 2 * n_z)),
            pltpu.SemaphoreType.DMA((ITERS, GROUPS, 2 * n_z)),
            pltpu.SemaphoreType.DMA((ITERS, GROUPS, n_col)),
            pltpu.SemaphoreType.DMA((ITERS, GROUPS, n_col)),
            pltpu.SemaphoreType.DMA((n_col,)),
            pltpu.SemaphoreType.DMA((n_col,)),
        ],
        compiler_params=pltpu.CompilerParams(
            collective_id=0, has_side_effects=True, vmem_limit_bytes=56 * 1024 * 1024
        ),
    )(labels_prior, tiles, tile_rows.reshape(1, -1), tile_cols.reshape(1, -1), tile_count)


def solution(mesh):
    n_row, n_col = mesh.shape["row"], mesh.shape["col"]
    in_specs = (
        P(None, ("row", "col")),
        P(("row", "col"), None, None),
        P(("row", "col")),
        P(("row", "col")),
        P(("row", "col")),
    )
    return jax.shard_map(
        functools.partial(local, n_row, n_col),
        mesh=mesh,
        in_specs=in_specs,
        out_specs=P(None, ("row", "col")),
        check_vma=False,
    )
```

```python
import functools

import jax
import jax.numpy as jnp
from jax import lax
from jax.experimental import pallas as pl
from jax.experimental.pallas import tpu as pltpu
from jax.sharding import PartitionSpec as P

ITERS = 2
SPREAD = 0.9
LEVELS = 65535.0
GROUPS = 2
LOADS = 7


def plan(rows, cols, count, table_ref, keep_ref, group_blocks):
    slots = rows.shape[1]
    lane = lax.broadcasted_iota(jnp.int32, (slots, slots), 1)
    down = lax.broadcasted_iota(jnp.int32, (slots, slots), 0)
    row = jnp.where(lane[0:1] < count, rows, group_blocks)
    key = row * slots + lane[0:1]
    same = lane == down

    def stand(x):
        return jnp.sum(jnp.where(same, x, 0), axis=1, keepdims=True)

    key_down, row_down, col_down = stand(key), stand(row), stand(cols)
    rank = jnp.sum((key < key_down).astype(jnp.int32), axis=1, keepdims=True)
    hit = rank == lane

    def lie(cond, x):
        return jnp.sum(jnp.where(cond, x, 0), axis=0, keepdims=True)

    here = lie(hit, row_down + 1)
    before = lie(rank + 1 == lane, row_down + 1)
    table_ref[0:1, 0:slots] = lie(hit, down)
    table_ref[1:2, 0:slots] = lie(hit, col_down)
    keep = stand((here == before).astype(jnp.int32)).astype(jnp.float32)
    keep_ref[...] = jnp.broadcast_to(keep, keep_ref.shape)
    group = lax.broadcasted_iota(jnp.int32, (slots, group_blocks), 1)
    stop = jnp.sum((row_down <= group).astype(jnp.int32), axis=0, keepdims=True)
    start = jnp.sum((row_down < group).astype(jnp.int32), axis=0, keepdims=True)
    table_ref[2:3, 0:group_blocks] = jnp.maximum(stop - 1, 0)
    table_ref[3:4, 0:group_blocks] = (stop > start).astype(jnp.int32)
    block = lax.broadcasted_iota(jnp.int32, (group_blocks, slots), 0)
    return (block == row).astype(jnp.float32)


def kernel(
    n_row, n_col,
    prior_hbm, tiles_hbm, slot_rows_hbm, slot_cols_hbm, count_hbm,
    out_ref,
    prior_ref, tiles_ref, ag_ref, upper_ref, lower_ref, run_ref, rows_ref, inv_ref, rows_in_ref, code_ref, code_in_ref,
    cur_ref, scale_ref, table_ref, plan_ref, keep_ref, slot_sum_ref, slots_ref, count_ref,
    prior_sem, load_sem, plan_sem, slots_sem, ag_send, ag_recv, rs_send, rs_recv, row_send, row_recv,
):
    labels, piece = prior_ref.shape
    slots, tile, _ = tiles_ref.shape
    own = piece // tile
    pairs = own // 2
    some = labels // GROUPS
    n_z = n_row // 2
    my_row = lax.axis_index("row")
    my_col = lax.axis_index("col")
    my_z = my_row // 2
    my_core = my_row % 2
    partner = my_z * 2 + (1 - my_core)

    def at(row, col):
        return {"row": row, "col": col}

    def part(g):
        return pl.ds(g * some, some)

    prior_copies = []
    for g in range(GROUPS):
        prior_copies.append(
            pltpu.make_async_copy(prior_hbm.at[part(g)], prior_ref.at[part(g)], prior_sem.at[g])
        )
        prior_copies[-1].start()

    barrier = pltpu.get_barrier_semaphore()
    z_to = [None] + [((my_z + d) % n_z) * 2 + my_core for d in range(1, n_z)]
    z_from = [None] + [((my_z + n_z - d) % n_z) * 2 + my_core for d in range(1, n_z)]
    p_from = [partner] + [((my_z + n_z - d) % n_z) * 2 + (1 - my_core) for d in range(1, n_z)]
    c_to = [None] + [(my_col + d) % n_col for d in range(1, n_col)]
    c_from = [None] + [(my_col + n_col - d) % n_col for d in range(1, n_col)]
    for d in range(1, n_z):
        pl.semaphore_signal(barrier, inc=1, device_id=at(z_to[d], my_col))
    pl.semaphore_signal(barrier, inc=1, device_id=at(partner, my_col))
    for d in range(1, n_col):
        pl.semaphore_signal(barrier, inc=1, device_id=at(my_row, c_to[d]))

    slot_copies = [
        pltpu.make_async_copy(slot_rows_hbm, slots_ref.at[0], slots_sem.at[0]),
        pltpu.make_async_copy(slot_cols_hbm, slots_ref.at[1], slots_sem.at[1]),
        pltpu.make_async_copy(count_hbm, count_ref, slots_sem.at[2]),
    ]
    for copy in slot_copies:
        copy.start()

    loads = []
    step = slots // LOADS
    for n in range(LOADS):
        window = pl.ds(n * step, step)
        loads.append(
            pltpu.make_async_copy(tiles_hbm.at[window], tiles_ref.at[window], load_sem.at[n])
        )
        loads[-1].start()

    sent = []

    def gather_copy(it, g, src_row, slot, to_row):
        window = pl.ds(src_row * pairs, pairs)
        return pltpu.make_async_remote_copy(
            src_ref=ag_ref.at[it, g, window],
            dst_ref=ag_ref.at[it, g, window],
            send_sem=ag_send.at[it, g, slot],
            recv_sem=ag_recv.at[it, g, slot],
            device_id=at(to_row, my_col),
        )

    def expand(it, g, src_row):
        def one(t, carry):
            both = ag_ref[it, g, src_row * pairs + t].astype(jnp.float32)
            blank = jnp.zeros((some, tile), jnp.float32)
            b = src_row * own + 2 * t
            for i, half in enumerate((both[:some], both[some:])):
                upper_ref[b + i] = jnp.concatenate([half, blank], axis=0).astype(jnp.bfloat16)
                lower_ref[b + i] = jnp.concatenate([blank, half], axis=0).astype(jnp.bfloat16)
            return carry

        lax.fori_loop(0, pairs, one, 0, unroll=True)

    def gather_start(it, g):
        copies = [gather_copy(it, g, my_row, d, z_to[d]) for d in range(1, n_z)]
        copies.append(gather_copy(it, g, my_row, n_z, partner))
        for copy in copies:
            copy.start()
        sent.extend(copies)

    def gather_finish(it, g):
        expand(it, g, my_row)
        for d in range(1, n_z):
            gather_copy(it, g, z_from[d], d, z_to[d]).wait_recv()
            copy = gather_copy(it, g, z_from[d], n_z + d, partner)
            copy.start()
            sent.append(copy)
        for d in range(1, n_z):
            expand(it, g, z_from[d])
        for d in range(n_z):
            gather_copy(it, g, p_from[d], n_z + d, partner).wait_recv()
            expand(it, g, p_from[d])

    def lanes(b):
        return pl.ds(pl.multiple_of(b * tile, tile), tile)

    for g in range(GROUPS):

        def round_prior(t, carry):
            both = [prior_ref[part(g), lanes(2 * t + i)] for i in range(2)]
            ag_ref[0, g, my_row * pairs + t] = jnp.concatenate(both, axis=0).astype(jnp.bfloat16)
            return carry

        prior_copies[g].wait()
        lax.fori_loop(0, pairs, round_prior, 0, unroll=True)
        if g == 0:
            pl.semaphore_wait(barrier, n_z + n_col - 1)
        gather_start(0, g)

    def product(left, right):
        return lax.dot_general(
            left, right, (((1,), (0,)), ((), ())), preferred_element_type=jnp.float32
        )

    for copy in slot_copies:
        copy.wait()
    hot = plan(slots_ref[0], slots_ref[1], count_ref[0], table_ref, keep_ref, n_col * own)
    plan_copy = pltpu.make_async_copy(table_ref, plan_ref, plan_sem)
    plan_copy.start()

    def weights(slot_pair):
        return jnp.concatenate([tiles_ref[n] for n in slot_pair], axis=0)

    down = lax.broadcasted_iota(jnp.int32, (2 * some, 2 * tile), 0)
    lane = lax.broadcasted_iota(jnp.int32, (2 * some, 2 * tile), 1)
    ones = ((down < some) == (lane < tile)).astype(jnp.float32).astype(jnp.bfloat16)
    for n, copy in enumerate(loads):
        copy.wait()

        def sum_pair(m, carry):
            k = n * step + 2 * m
            for turned in (k, k + 1):
                tiles_ref[turned] = tiles_ref[turned].T
            both = product(ones, weights((k, k + 1)))
            for i in range(2):
                slot_sum_ref[pl.ds(k + i, 1), :] = both[i * some : i * some + 1]
            return carry

        lax.fori_loop(0, step // 2, sum_pair, 0, unroll=True)
    rows_ref[...] = jnp.dot(
        hot, slot_sum_ref[...], precision=lax.Precision.HIGHEST, preferred_element_type=jnp.float32
    )

    def row_copy(d):
        return pltpu.make_async_remote_copy(
            src_ref=rows_ref.at[pl.ds(pl.multiple_of(c_to[d] * own, own), own)],
            dst_ref=rows_in_ref.at[d],
            send_sem=row_send.at[d],
            recv_sem=row_recv.at[d],
            device_id=at(my_row, c_to[d]),
        )

    for d in range(1, n_col):
        copy = row_copy(d)
        copy.start()
        sent.append(copy)
    whole = rows_ref[...]
    inv_ref[...] = jnp.where(whole > 0.0, LEVELS / jnp.where(whole > 0.0, whole, 1.0), 0.0)
    plan_copy.wait()

    def code_copy(it, g, d):
        return pltpu.make_async_remote_copy(
            src_ref=code_ref.at[it, g, pl.ds(c_to[d] * pairs, pairs)],
            dst_ref=code_in_ref.at[it, g, d],
            send_sem=rs_send.at[it, g, d],
            recv_sem=rs_recv.at[it, g, d],
            device_id=at(my_row, c_to[d]),
        )

    def multiply(it, g):
        def add_pair(m, total):
            ks = (2 * m, 2 * m + 1)
            left = jnp.concatenate(
                [upper_ref[plan_ref[1, ks[0]]], lower_ref[plan_ref[1, ks[1]]]], axis=1
            )
            both = product(left, weights([plan_ref[0, k] for k in ks]))
            for i, k in enumerate(ks):
                keep = jnp.broadcast_to(keep_ref[pl.ds(k, 1), :], (some, tile))
                total = total * keep + both[i * some : (i + 1) * some]
                run_ref[g, k] = total
            return total

        lax.fori_loop(0, slots // 2, add_pair, jnp.zeros((some, tile), jnp.float32), unroll=True)

    def send_codes(it, g):
        for d in range(1, n_col):

            def encode(t, carry):
                levels = []
                for i in range(2):
                    r = c_to[d] * own + 2 * t + i
                    value = run_ref[g, plan_ref[2, r]]
                    levels.append(jnp.minimum(value * inv_ref[pl.ds(r, 1), :] + 0.5, LEVELS))
                level = jnp.concatenate(levels, axis=0).astype(jnp.int32) - 32768
                code_ref[it, g, c_to[d] * pairs + t] = level.astype(jnp.int16)
                return carry

            lax.fori_loop(0, pairs, encode, 0, unroll=True)
            copy = code_copy(it, g, d)
            copy.start()
            sent.append(copy)

    def update(it, g):
        for d in range(1, n_col):
            code_copy(it, g, d).wait_recv()

        def one(t, carry):
            found = [
                code_in_ref[it, g, d, t].astype(jnp.int32).astype(jnp.float32) + 32768.0
                for d in range(1, n_col)
            ]
            values = []
            for i in range(2):
                b = 2 * t + i
                r = my_col * own + b
                prior = prior_ref[part(g), lanes(b)]
                total = prior if it == 0 else cur_ref[g, b]
                total = total + run_ref[g, plan_ref[2, r]] * plan_ref[3, r].astype(jnp.float32)
                for d in range(1, n_col):
                    level = found[d - 1][i * some : (i + 1) * some]
                    total = total + level * (rows_in_ref[d, pl.ds(b, 1), :] * (1.0 / LEVELS))
                value = total * scale_ref[pl.ds(b, 1), :] + (1.0 - SPREAD) * prior
                if it + 1 < ITERS:
                    cur_ref[g, b] = value
                    values.append(value)
                else:
                    out_ref[part(g), lanes(b)] = value
            if it + 1 < ITERS:
                ag_ref[it + 1, g, my_row * pairs + t] = jnp.concatenate(values, axis=0).astype(jnp.bfloat16)
            return carry

        lax.fori_loop(0, pairs, one, 0, unroll=True)

    for it in range(ITERS):
        for g in range(GROUPS):
            gather_finish(it, g)
            multiply(it, g)
            send_codes(it, g)
        if it == 0:
            degree = 1.0 + rows_ref[pl.ds(pl.multiple_of(my_col * own, own), own), :]
            for d in range(1, n_col):
                row_copy(d).wait_recv()
                degree = degree + rows_in_ref[d]
            scale_ref[...] = SPREAD / degree
        for g in range(GROUPS):
            update(it, g)
            if it + 1 < ITERS:
                gather_start(it + 1, g)

    for copy in sent:
        copy.wait_send()


def local(n_row, n_col, labels_prior, tiles, tile_rows, tile_cols, tile_count):
    labels, piece = labels_prior.shape
    slots, tile, _ = tiles.shape
    own = piece // tile
    pairs = own // 2
    some = labels // GROUPS
    n_z = n_row // 2
    group = n_col * own
    width = -(-max(slots, group) // 128) * 128
    vmem = pl.BlockSpec(memory_space=pltpu.VMEM)
    return pl.pallas_call(
        functools.partial(kernel, n_row, n_col),
        out_shape=pltpu.VMEM((labels, piece), jnp.float32),
        in_specs=[pl.BlockSpec(memory_space=pl.ANY)] * 5,
        out_specs=vmem,
        scratch_shapes=[
            pltpu.VMEM((labels, piece), jnp.float32),
            pltpu.VMEM((slots, tile, tile), jnp.bfloat16),
            pltpu.VMEM((ITERS, GROUPS, n_row * pairs, 2 * some, tile), jnp.bfloat16),
            pltpu.VMEM((n_row * own, 2 * some, tile), jnp.bfloat16),
            pltpu.VMEM((n_row * own, 2 * some, tile), jnp.bfloat16),
            pltpu.VMEM((GROUPS, slots, some, tile), jnp.float32),
            pltpu.VMEM((group, tile), jnp.float32),
            pltpu.VMEM((group, tile), jnp.float32),
            pltpu.VMEM((n_col, own, tile), jnp.float32),
            pltpu.VMEM((ITERS, GROUPS, n_col * pairs, 2 * some, tile), jnp.int16),
            pltpu.VMEM((ITERS, GROUPS, n_col, pairs, 2 * some, tile), jnp.int16),
            pltpu.VMEM((GROUPS, own, some, tile), jnp.float32),
            pltpu.VMEM((own, tile), jnp.float32),
            pltpu.VMEM((8, width), jnp.int32),
            pltpu.SMEM((8, width), jnp.int32),
            pltpu.VMEM((slots, tile), jnp.float32),
            pltpu.VMEM((slots, tile), jnp.float32),
            pltpu.VMEM((2, 1, slots), jnp.int32),
            pltpu.SMEM((1,), jnp.int32),
            pltpu.SemaphoreType.DMA((GROUPS,)),
            pltpu.SemaphoreType.DMA((LOADS,)),
            pltpu.SemaphoreType.DMA(()),
            pltpu.SemaphoreType.DMA((3,)),
            pltpu.SemaphoreType.DMA((ITERS, GROUPS, 2 * n_z)),
            pltpu.SemaphoreType.DMA((ITERS, GROUPS, 2 * n_z)),
            pltpu.SemaphoreType.DMA((ITERS, GROUPS, n_col)),
            pltpu.SemaphoreType.DMA((ITERS, GROUPS, n_col)),
            pltpu.SemaphoreType.DMA((n_col,)),
            pltpu.SemaphoreType.DMA((n_col,)),
        ],
        compiler_params=pltpu.CompilerParams(
            collective_id=0, has_side_effects=True, vmem_limit_bytes=56 * 1024 * 1024
        ),
    )(labels_prior, tiles, tile_rows.reshape(1, -1), tile_cols.reshape(1, -1), tile_count)


def solution(mesh):
    n_row, n_col = mesh.shape["row"], mesh.shape["col"]
    in_specs = (
        P(None, ("row", "col")),
        P(("row", "col"), None, None),
        P(("row", "col")),
        P(("row", "col")),
        P(("row", "col")),
    )
    return jax.shard_map(
        functools.partial(local, n_row, n_col),
        mesh=mesh,
        in_specs=in_specs,
        out_specs=P(None, ("row", "col")),
        check_vma=False,
    )
```

```python
import functools

import jax
import jax.numpy as jnp
from jax import lax
from jax.experimental import pallas as pl
from jax.experimental.pallas import tpu as pltpu
from jax.sharding import PartitionSpec as P

ITERS = 2
SPREAD = 0.9
LEVELS = 65535.0
GROUPS = 2
LOADS = 7
LATE = (ITERS - 1,)


def plan(rows, cols, count, table_ref, keep_ref, group_blocks):
    slots = rows.shape[1]
    lane = lax.broadcasted_iota(jnp.int32, (slots, slots), 1)
    down = lax.broadcasted_iota(jnp.int32, (slots, slots), 0)
    row = jnp.where(lane[0:1] < count, rows, group_blocks)
    key = row * slots + lane[0:1]
    same = lane == down

    def stand(x):
        return jnp.sum(jnp.where(same, x, 0), axis=1, keepdims=True)

    key_down, row_down, col_down = stand(key), stand(row), stand(cols)
    rank = jnp.sum((key < key_down).astype(jnp.int32), axis=1, keepdims=True)
    hit = rank == lane

    def lie(cond, x):
        return jnp.sum(jnp.where(cond, x, 0), axis=0, keepdims=True)

    here = lie(hit, row_down + 1)
    before = lie(rank + 1 == lane, row_down + 1)
    table_ref[0:1, 0:slots] = lie(hit, down)
    table_ref[1:2, 0:slots] = lie(hit, col_down)
    keep = stand((here == before).astype(jnp.int32)).astype(jnp.float32)
    keep_ref[...] = jnp.broadcast_to(keep, keep_ref.shape)
    group = lax.broadcasted_iota(jnp.int32, (slots, group_blocks), 1)
    stop = jnp.sum((row_down <= group).astype(jnp.int32), axis=0, keepdims=True)
    start = jnp.sum((row_down < group).astype(jnp.int32), axis=0, keepdims=True)
    table_ref[2:3, 0:group_blocks] = jnp.maximum(stop - 1, 0)
    table_ref[3:4, 0:group_blocks] = (stop > start).astype(jnp.int32)
    block = lax.broadcasted_iota(jnp.int32, (group_blocks, slots), 0)
    return (block == row).astype(jnp.float32)


def kernel(
    n_row, n_col,
    prior_hbm, tiles_hbm, slot_rows_hbm, slot_cols_hbm, count_hbm,
    out_ref,
    prior_ref, tiles_ref, ag_ref, upper_ref, lower_ref, run_ref, rows_ref, inv_ref, rows_in_ref, code_ref, code_in_ref,
    cur_ref, scale_ref, table_ref, plan_ref, keep_ref, slot_sum_ref, slots_ref, count_ref,
    prior_sem, load_sem, plan_sem, slots_sem, ag_send, ag_recv, rs_send, rs_recv, row_send, row_recv,
):
    labels, piece = prior_ref.shape
    slots, tile, _ = tiles_ref.shape
    own = piece // tile
    pairs = own // 2
    some = labels // GROUPS
    n_z = n_row // 2
    my_row = lax.axis_index("row")
    my_col = lax.axis_index("col")
    my_z = my_row // 2
    my_core = my_row % 2
    partner = my_z * 2 + (1 - my_core)

    def at(row, col):
        return {"row": row, "col": col}

    def part(g):
        return pl.ds(g * some, some)

    prior_copies = []
    for g in range(GROUPS):
        prior_copies.append(
            pltpu.make_async_copy(prior_hbm.at[part(g)], prior_ref.at[part(g)], prior_sem.at[g])
        )
        prior_copies[-1].start()

    barrier = pltpu.get_barrier_semaphore()
    z_to = [None] + [((my_z + d) % n_z) * 2 + my_core for d in range(1, n_z)]
    z_from = [None] + [((my_z + n_z - d) % n_z) * 2 + my_core for d in range(1, n_z)]
    asc = [None] + [(d - 1 + jnp.where(d - 1 < my_z, 0, 1)) * 2 + my_core for d in range(1, n_z)]
    p_from = [partner] + [((my_z + n_z - d) % n_z) * 2 + (1 - my_core) for d in range(1, n_z)]
    c_to = [None] + [(my_col + d) % n_col for d in range(1, n_col)]
    c_from = [None] + [(my_col + n_col - d) % n_col for d in range(1, n_col)]
    for d in range(1, n_z):
        pl.semaphore_signal(barrier, inc=1, device_id=at(z_to[d], my_col))
    pl.semaphore_signal(barrier, inc=1, device_id=at(partner, my_col))
    for d in range(1, n_col):
        pl.semaphore_signal(barrier, inc=1, device_id=at(my_row, c_to[d]))

    slot_copies = [
        pltpu.make_async_copy(slot_rows_hbm, slots_ref.at[0], slots_sem.at[0]),
        pltpu.make_async_copy(slot_cols_hbm, slots_ref.at[1], slots_sem.at[1]),
        pltpu.make_async_copy(count_hbm, count_ref, slots_sem.at[2]),
    ]
    for copy in slot_copies:
        copy.start()

    loads = []
    step = slots // LOADS
    for n in range(LOADS):
        window = pl.ds(n * step, step)
        loads.append(
            pltpu.make_async_copy(tiles_hbm.at[window], tiles_ref.at[window], load_sem.at[n])
        )
        loads[-1].start()

    sent = []

    def gather_copy(it, g, src_row, slot, to_row):
        window = pl.ds(src_row * pairs, pairs)
        return pltpu.make_async_remote_copy(
            src_ref=ag_ref.at[it, g, window],
            dst_ref=ag_ref.at[it, g, window],
            send_sem=ag_send.at[it, g, slot],
            recv_sem=ag_recv.at[it, g, (slot // n_z) * n_z + src_row // 2],
            device_id=at(to_row, my_col),
        )

    def expand(it, g, src_row):
        def one(t, carry):
            both = ag_ref[it, g, src_row * pairs + t].astype(jnp.float32)
            blank = jnp.zeros((some, tile), jnp.float32)
            b = src_row * own + 2 * t
            for i, half in enumerate((both[:some], both[some:])):
                upper_ref[b + i] = jnp.concatenate([half, blank], axis=0).astype(jnp.bfloat16)
                lower_ref[b + i] = jnp.concatenate([blank, half], axis=0).astype(jnp.bfloat16)
            return carry

        lax.fori_loop(0, pairs, one, 0, unroll=True)

    def gather_start(it, g):
        copies = [gather_copy(it, g, my_row, n_z, partner)]
        to = asc if it + 1 == ITERS else z_to
        copies += [gather_copy(it, g, my_row, d, to[d]) for d in range(1, n_z)]
        for copy in copies:
            copy.start()
        sent.extend(copies)

    def gather_pass(it, g, d):
        gather_copy(it, g, z_from[d], d, z_to[d]).wait_recv()
        copy = gather_copy(it, g, z_from[d], n_z + d, partner)
        copy.start()
        sent.append(copy)

    def gather_finish(it, g, passed=False):
        expand(it, g, my_row)
        for d in range(1, n_z):
            if not passed:
                gather_pass(it, g, d)
        for d in range(1, n_z):
            expand(it, g, z_from[d])
        for d in range(n_z):
            gather_copy(it, g, p_from[d], n_z + d, partner).wait_recv()
            expand(it, g, p_from[d])

    def lanes(b):
        return pl.ds(pl.multiple_of(b * tile, tile), tile)

    for g in range(GROUPS):

        def round_prior(t, carry):
            both = [prior_ref[part(g), lanes(2 * t + i)] for i in range(2)]
            ag_ref[0, g, my_row * pairs + t] = jnp.concatenate(both, axis=0).astype(jnp.bfloat16)
            return carry

        prior_copies[g].wait()
        lax.fori_loop(0, pairs, round_prior, 0, unroll=True)
        if g == 0:
            pl.semaphore_wait(barrier, n_z + n_col - 1)
        gather_start(0, g)

    def product(left, right):
        return lax.dot_general(
            left, right, (((1,), (0,)), ((), ())), preferred_element_type=jnp.float32
        )

    for copy in slot_copies:
        copy.wait()
    hot = plan(slots_ref[0], slots_ref[1], count_ref[0], table_ref, keep_ref, n_col * own)
    plan_copy = pltpu.make_async_copy(table_ref, plan_ref, plan_sem)
    plan_copy.start()

    def weights(slot_pair):
        return jnp.concatenate([tiles_ref[n] for n in slot_pair], axis=0)

    down = lax.broadcasted_iota(jnp.int32, (2 * some, 2 * tile), 0)
    lane = lax.broadcasted_iota(jnp.int32, (2 * some, 2 * tile), 1)
    ones = ((down < some) == (lane < tile)).astype(jnp.float32).astype(jnp.bfloat16)
    for n, copy in enumerate(loads):
        copy.wait()

        def sum_pair(m, carry):
            k = n * step + 2 * m
            for turned in (k, k + 1):
                tiles_ref[turned] = tiles_ref[turned].T
            both = product(ones, weights((k, k + 1)))
            for i in range(2):
                slot_sum_ref[pl.ds(k + i, 1), :] = both[i * some : i * some + 1]
            return carry

        lax.fori_loop(0, step // 2, sum_pair, 0, unroll=True)
    rows_ref[...] = jnp.dot(
        hot, slot_sum_ref[...], precision=lax.Precision.HIGHEST, preferred_element_type=jnp.float32
    )

    def row_copy(d):
        return pltpu.make_async_remote_copy(
            src_ref=rows_ref.at[pl.ds(pl.multiple_of(c_to[d] * own, own), own)],
            dst_ref=rows_in_ref.at[d],
            send_sem=row_send.at[d],
            recv_sem=row_recv.at[d],
            device_id=at(my_row, c_to[d]),
        )

    for d in range(1, n_col):
        copy = row_copy(d)
        copy.start()
        sent.append(copy)
    whole = rows_ref[...]
    inv_ref[...] = jnp.where(whole > 0.0, LEVELS / jnp.where(whole > 0.0, whole, 1.0), 0.0)
    plan_copy.wait()

    def code_copy(it, g, d, to):
        return pltpu.make_async_remote_copy(
            src_ref=code_ref.at[it, g, pl.ds(to * pairs, pairs)],
            dst_ref=code_in_ref.at[it, g, d],
            send_sem=rs_send.at[it, g, d],
            recv_sem=rs_recv.at[it, g, d],
            device_id=at(my_row, to),
        )

    def multiply(it, g):
        def add_pair(m, total):
            ks = (2 * m, 2 * m + 1)
            left = jnp.concatenate(
                [upper_ref[plan_ref[1, ks[0]]], lower_ref[plan_ref[1, ks[1]]]], axis=1
            )
            both = product(left, weights([plan_ref[0, k] for k in ks]))
            for i, k in enumerate(ks):
                keep = jnp.broadcast_to(keep_ref[pl.ds(k, 1), :], (some, tile))
                total = total * keep + both[i * some : (i + 1) * some]
                run_ref[g, k] = total
            return total

        lax.fori_loop(0, slots // 2, add_pair, jnp.zeros((some, tile), jnp.float32), unroll=True)

    def send_codes(it, g):
        for i in range(1, n_col):
            to = c_to[i]
            d = i
            if it + 1 == ITERS:
                to = i - 1 + jnp.where(i - 1 < my_col, 0, 1)
                d = (to + n_col - my_col) % n_col


            def encode(t, carry):
                levels = []
                for i in range(2):
                    r = to * own + 2 * t + i
                    value = run_ref[g, plan_ref[2, r]]
                    levels.append(jnp.minimum(value * inv_ref[pl.ds(r, 1), :] + 0.5, LEVELS))
                level = jnp.concatenate(levels, axis=0).astype(jnp.int32) - 32768
                code_ref[it, g, to * pairs + t] = level.astype(jnp.int16)
                return carry

            lax.fori_loop(0, pairs, encode, 0, unroll=True)
            copy = code_copy(it, g, d, to)
            copy.start()
            sent.append(copy)

    def update(it, g):
        for d in range(1, n_col):
            code_copy(it, g, d, c_to[d]).wait_recv()

        def one(t, carry):
            found = [
                code_in_ref[it, g, d, t].astype(jnp.int32).astype(jnp.float32) + 32768.0
                for d in range(1, n_col)
            ]
            values = []
            for i in range(2):
                b = 2 * t + i
                r = my_col * own + b
                prior = prior_ref[part(g), lanes(b)]
                total = prior if it == 0 else cur_ref[g, b]
                total = total + run_ref[g, plan_ref[2, r]] * plan_ref[3, r].astype(jnp.float32)
                for d in range(1, n_col):
                    level = found[d - 1][i * some : (i + 1) * some]
                    total = total + level * (rows_in_ref[d, pl.ds(b, 1), :] * (1.0 / LEVELS))
                value = total * scale_ref[pl.ds(b, 1), :] + (1.0 - SPREAD) * prior
                if it + 1 < ITERS:
                    cur_ref[g, b] = value
                    values.append(value)
                else:
                    out_ref[part(g), lanes(b)] = value
            if it + 1 < ITERS:
                ag_ref[it + 1, g, my_row * pairs + t] = jnp.concatenate(values, axis=0).astype(jnp.bfloat16)
            return carry

        lax.fori_loop(0, pairs, one, 0, unroll=True)

    for it in range(ITERS):
        for g in range(GROUPS):
            gather_finish(it, g, passed=it in LATE and g > 0)
            multiply(it, g)
            if it in LATE and g + 1 < GROUPS:
                for d in range(1, n_z):
                    gather_pass(it, g + 1, d)
            send_codes(it, g)
        if it == 0:
            degree = 1.0 + rows_ref[pl.ds(pl.multiple_of(my_col * own, own), own), :]
            for d in range(1, n_col):
                row_copy(d).wait_recv()
                degree = degree + rows_in_ref[d]
            scale_ref[...] = SPREAD / degree
        for g in range(GROUPS):
            update(it, g)
            if it + 1 < ITERS:
                gather_start(it + 1, g)

    for copy in sent:
        copy.wait_send()


def local(n_row, n_col, labels_prior, tiles, tile_rows, tile_cols, tile_count):
    labels, piece = labels_prior.shape
    slots, tile, _ = tiles.shape
    own = piece // tile
    pairs = own // 2
    some = labels // GROUPS
    n_z = n_row // 2
    group = n_col * own
    width = -(-max(slots, group) // 128) * 128
    vmem = pl.BlockSpec(memory_space=pltpu.VMEM)
    return pl.pallas_call(
        functools.partial(kernel, n_row, n_col),
        out_shape=pltpu.VMEM((labels, piece), jnp.float32),
        in_specs=[pl.BlockSpec(memory_space=pl.ANY)] * 5,
        out_specs=vmem,
        scratch_shapes=[
            pltpu.VMEM((labels, piece), jnp.float32),
            pltpu.VMEM((slots, tile, tile), jnp.bfloat16),
            pltpu.VMEM((ITERS, GROUPS, n_row * pairs, 2 * some, tile), jnp.bfloat16),
            pltpu.VMEM((n_row * own, 2 * some, tile), jnp.bfloat16),
            pltpu.VMEM((n_row * own, 2 * some, tile), jnp.bfloat16),
            pltpu.VMEM((GROUPS, slots, some, tile), jnp.float32),
            pltpu.VMEM((group, tile), jnp.float32),
            pltpu.VMEM((group, tile), jnp.float32),
            pltpu.VMEM((n_col, own, tile), jnp.float32),
            pltpu.VMEM((ITERS, GROUPS, n_col * pairs, 2 * some, tile), jnp.int16),
            pltpu.VMEM((ITERS, GROUPS, n_col, pairs, 2 * some, tile), jnp.int16),
            pltpu.VMEM((GROUPS, own, some, tile), jnp.float32),
            pltpu.VMEM((own, tile), jnp.float32),
            pltpu.VMEM((8, width), jnp.int32),
            pltpu.SMEM((8, width), jnp.int32),
            pltpu.VMEM((slots, tile), jnp.float32),
            pltpu.VMEM((slots, tile), jnp.float32),
            pltpu.VMEM((2, 1, slots), jnp.int32),
            pltpu.SMEM((1,), jnp.int32),
            pltpu.SemaphoreType.DMA((GROUPS,)),
            pltpu.SemaphoreType.DMA((LOADS,)),
            pltpu.SemaphoreType.DMA(()),
            pltpu.SemaphoreType.DMA((3,)),
            pltpu.SemaphoreType.DMA((ITERS, GROUPS, 2 * n_z)),
            pltpu.SemaphoreType.DMA((ITERS, GROUPS, 2 * n_z)),
            pltpu.SemaphoreType.DMA((ITERS, GROUPS, n_col)),
            pltpu.SemaphoreType.DMA((ITERS, GROUPS, n_col)),
            pltpu.SemaphoreType.DMA((n_col,)),
            pltpu.SemaphoreType.DMA((n_col,)),
        ],
        compiler_params=pltpu.CompilerParams(
            collective_id=0, has_side_effects=True, vmem_limit_bytes=56 * 1024 * 1024
        ),
    )(labels_prior, tiles, tile_rows.reshape(1, -1), tile_cols.reshape(1, -1), tile_count)


def solution(mesh):
    n_row, n_col = mesh.shape["row"], mesh.shape["col"]
    in_specs = (
        P(None, ("row", "col")),
        P(("row", "col"), None, None),
        P(("row", "col")),
        P(("row", "col")),
        P(("row", "col")),
    )
    return jax.shard_map(
        functools.partial(local, n_row, n_col),
        mesh=mesh,
        in_specs=in_specs,
        out_specs=P(None, ("row", "col")),
        check_vma=False,
    )
```

```python
import functools

import jax
import jax.numpy as jnp
from jax import lax
from jax.experimental import pallas as pl
from jax.experimental.pallas import tpu as pltpu
from jax.sharding import PartitionSpec as P

ITERS = 2
SPREAD = 0.9
LEVELS = 65535.0
GROUPS = 2
LOADS = 4
LATE = (ITERS - 1,)


def plan(rows, cols, count, table_ref, keep_ref, group_blocks):
    slots = rows.shape[1]
    lane = lax.broadcasted_iota(jnp.int32, (slots, slots), 1)
    down = lax.broadcasted_iota(jnp.int32, (slots, slots), 0)
    row = jnp.where(lane[0:1] < count, rows, group_blocks)
    key = row * slots + lane[0:1]
    same = lane == down

    def stand(x):
        return jnp.sum(jnp.where(same, x, 0), axis=1, keepdims=True)

    key_down, row_down, col_down = stand(key), stand(row), stand(cols)
    rank = jnp.sum((key < key_down).astype(jnp.int32), axis=1, keepdims=True)
    hit = rank == lane

    def lie(cond, x):
        return jnp.sum(jnp.where(cond, x, 0), axis=0, keepdims=True)

    here = lie(hit, row_down + 1)
    before = lie(rank + 1 == lane, row_down + 1)
    table_ref[0:1, 0:slots] = lie(hit, down)
    table_ref[1:2, 0:slots] = lie(hit, col_down)
    keep = stand((here == before).astype(jnp.int32)).astype(jnp.float32)
    keep_ref[...] = jnp.broadcast_to(keep, keep_ref.shape)
    group = lax.broadcasted_iota(jnp.int32, (slots, group_blocks), 1)
    stop = jnp.sum((row_down <= group).astype(jnp.int32), axis=0, keepdims=True)
    start = jnp.sum((row_down < group).astype(jnp.int32), axis=0, keepdims=True)
    table_ref[2:3, 0:group_blocks] = jnp.maximum(stop - 1, 0)
    table_ref[3:4, 0:group_blocks] = (stop > start).astype(jnp.int32)
    block = lax.broadcasted_iota(jnp.int32, (group_blocks, slots), 0)
    return (block == row).astype(jnp.float32)


def kernel(
    n_row, n_col,
    prior_hbm, tiles_hbm, slot_rows_hbm, slot_cols_hbm, count_hbm,
    out_ref,
    prior_ref, tiles_ref, ag_ref, upper_ref, lower_ref, run_ref, rows_ref, inv_ref, rows_in_ref, code_ref, code_in_ref,
    cur_ref, scale_ref, table_ref, plan_ref, keep_ref, slot_sum_ref, slots_ref, count_ref,
    prior_sem, load_sem, plan_sem, slots_sem, ag_send, ag_recv, rs_send, rs_recv, row_send, row_recv,
):
    labels, piece = prior_ref.shape
    slots, tile, _ = tiles_ref.shape
    own = piece // tile
    pairs = own // 2
    some = labels // GROUPS
    n_z = n_row // 2
    my_row = lax.axis_index("row")
    my_col = lax.axis_index("col")
    my_z = my_row // 2
    my_core = my_row % 2
    partner = my_z * 2 + (1 - my_core)

    def at(row, col):
        return {"row": row, "col": col}

    def part(g):
        return pl.ds(g * some, some)

    prior_copies = []
    for g in range(GROUPS):
        prior_copies.append(
            pltpu.make_async_copy(prior_hbm.at[part(g)], prior_ref.at[part(g)], prior_sem.at[g])
        )
        prior_copies[-1].start()

    barrier = pltpu.get_barrier_semaphore()
    z_to = [None] + [((my_z + d) % n_z) * 2 + my_core for d in range(1, n_z)]
    z_from = [None] + [((my_z + n_z - d) % n_z) * 2 + my_core for d in range(1, n_z)]
    asc = [None] + [(d - 1 + jnp.where(d - 1 < my_z, 0, 1)) * 2 + my_core for d in range(1, n_z)]
    p_from = [partner] + [((my_z + n_z - d) % n_z) * 2 + (1 - my_core) for d in range(1, n_z)]
    c_to = [None] + [(my_col + d) % n_col for d in range(1, n_col)]
    c_from = [None] + [(my_col + n_col - d) % n_col for d in range(1, n_col)]
    for d in range(1, n_z):
        pl.semaphore_signal(barrier, inc=1, device_id=at(z_to[d], my_col))
    pl.semaphore_signal(barrier, inc=1, device_id=at(partner, my_col))
    for d in range(1, n_col):
        pl.semaphore_signal(barrier, inc=1, device_id=at(my_row, c_to[d]))

    slot_copies = [
        pltpu.make_async_copy(slot_rows_hbm, slots_ref.at[0], slots_sem.at[0]),
        pltpu.make_async_copy(slot_cols_hbm, slots_ref.at[1], slots_sem.at[1]),
        pltpu.make_async_copy(count_hbm, count_ref, slots_sem.at[2]),
    ]
    for copy in slot_copies:
        copy.start()

    loads = []
    step = slots // LOADS
    for n in range(LOADS):
        window = pl.ds(n * step, step)
        loads.append(
            pltpu.make_async_copy(tiles_hbm.at[window], tiles_ref.at[window], load_sem.at[n])
        )
        loads[-1].start()

    sent = []

    def gather_copy(it, g, src_row, slot, to_row):
        window = pl.ds(src_row * pairs, pairs)
        return pltpu.make_async_remote_copy(
            src_ref=ag_ref.at[it, g, window],
            dst_ref=ag_ref.at[it, g, window],
            send_sem=ag_send.at[it, g, slot],
            recv_sem=ag_recv.at[it, g, (slot // n_z) * n_z + src_row // 2],
            device_id=at(to_row, my_col),
        )

    def expand(it, g, src_row):
        def one(t, carry):
            both = ag_ref[it, g, src_row * pairs + t].astype(jnp.float32)
            blank = jnp.zeros((some, tile), jnp.float32)
            b = src_row * own + 2 * t
            for i, half in enumerate((both[:some], both[some:])):
                upper_ref[b + i] = jnp.concatenate([half, blank], axis=0).astype(jnp.bfloat16)
                lower_ref[b + i] = jnp.concatenate([blank, half], axis=0).astype(jnp.bfloat16)
            return carry

        lax.fori_loop(0, pairs, one, 0, unroll=True)

    def gather_start(it, g):
        copies = [gather_copy(it, g, my_row, n_z, partner)]
        to = asc if it + 1 == ITERS else z_to
        copies += [gather_copy(it, g, my_row, d, to[d]) for d in range(1, n_z)]
        for copy in copies:
            copy.start()
        sent.extend(copies)

    def gather_pass(it, g, d):
        gather_copy(it, g, z_from[d], d, z_to[d]).wait_recv()
        copy = gather_copy(it, g, z_from[d], n_z + d, partner)
        copy.start()
        sent.append(copy)

    def gather_finish(it, g, passed=False):
        for d in range(1, n_z):
            if not passed:
                gather_pass(it, g, d)
        expand(it, g, my_row)
        for d in range(1, n_z):
            expand(it, g, z_from[d])
        for d in range(n_z):
            gather_copy(it, g, p_from[d], n_z + d, partner).wait_recv()
            expand(it, g, p_from[d])

    def lanes(b):
        return pl.ds(pl.multiple_of(b * tile, tile), tile)

    for g in range(GROUPS):

        def round_prior(t, carry):
            both = [prior_ref[part(g), lanes(2 * t + i)] for i in range(2)]
            ag_ref[0, g, my_row * pairs + t] = jnp.concatenate(both, axis=0).astype(jnp.bfloat16)
            return carry

        prior_copies[g].wait()
        lax.fori_loop(0, pairs, round_prior, 0, unroll=True)
        if g == 0:
            pl.semaphore_wait(barrier, n_z + n_col - 1)
        gather_start(0, g)

    def product(left, right):
        return lax.dot_general(
            left, right, (((1,), (0,)), ((), ())), preferred_element_type=jnp.float32
        )

    for copy in slot_copies:
        copy.wait()
    hot = plan(slots_ref[0], slots_ref[1], count_ref[0], table_ref, keep_ref, n_col * own)
    plan_copy = pltpu.make_async_copy(table_ref, plan_ref, plan_sem)
    plan_copy.start()

    def weights(slot_pair):
        return jnp.concatenate([tiles_ref[n] for n in slot_pair], axis=0)

    down = lax.broadcasted_iota(jnp.int32, (2 * some, 2 * tile), 0)
    lane = lax.broadcasted_iota(jnp.int32, (2 * some, 2 * tile), 1)
    ones = ((down < some) == (lane < tile)).astype(jnp.float32).astype(jnp.bfloat16)
    for n, copy in enumerate(loads):
        copy.wait()

        def sum_pair(m, carry):
            k = n * step + 2 * m
            for turned in (k, k + 1):
                tiles_ref[turned] = tiles_ref[turned].T
            both = product(ones, weights((k, k + 1)))
            for i in range(2):
                slot_sum_ref[pl.ds(k + i, 1), :] = both[i * some : i * some + 1]
            return carry

        lax.fori_loop(0, step // 2, sum_pair, 0, unroll=True)
    rows_ref[...] = jnp.dot(
        hot, slot_sum_ref[...], precision=lax.Precision.HIGHEST, preferred_element_type=jnp.float32
    )

    def row_copy(d):
        return pltpu.make_async_remote_copy(
            src_ref=rows_ref.at[pl.ds(pl.multiple_of(c_to[d] * own, own), own)],
            dst_ref=rows_in_ref.at[d],
            send_sem=row_send.at[d],
            recv_sem=row_recv.at[d],
            device_id=at(my_row, c_to[d]),
        )

    for d in range(1, n_col):
        copy = row_copy(d)
        copy.start()
        sent.append(copy)
    whole = rows_ref[...]
    inv_ref[...] = jnp.where(whole > 0.0, LEVELS / jnp.where(whole > 0.0, whole, 1.0), 0.0)
    plan_copy.wait()

    def code_copy(it, g, d, to):
        return pltpu.make_async_remote_copy(
            src_ref=code_ref.at[it, g, pl.ds(to * pairs, pairs)],
            dst_ref=code_in_ref.at[it, g, d],
            send_sem=rs_send.at[it, g, d],
            recv_sem=rs_recv.at[it, g, d],
            device_id=at(my_row, to),
        )

    def multiply(it, g):
        def add_pair(m, total):
            ks = (2 * m, 2 * m + 1)
            left = jnp.concatenate(
                [upper_ref[plan_ref[1, ks[0]]], lower_ref[plan_ref[1, ks[1]]]], axis=1
            )
            both = product(left, weights([plan_ref[0, k] for k in ks]))
            for i, k in enumerate(ks):
                keep = jnp.broadcast_to(keep_ref[pl.ds(k, 1), :], (some, tile))
                total = total * keep + both[i * some : (i + 1) * some]
                run_ref[g, k] = total
            return total

        lax.fori_loop(0, slots // 2, add_pair, jnp.zeros((some, tile), jnp.float32), unroll=True)

    def send_codes(it, g):
        for i in range(1, n_col):
            to = c_to[i]
            d = i
            if it + 1 == ITERS:
                to = i - 1 + jnp.where(i - 1 < my_col, 0, 1)
                d = (to + n_col - my_col) % n_col


            def encode(t, carry):
                levels = []
                for i in range(2):
                    r = to * own + 2 * t + i
                    value = run_ref[g, plan_ref[2, r]]
                    levels.append(jnp.minimum(value * inv_ref[pl.ds(r, 1), :] + 0.5, LEVELS))
                level = jnp.concatenate(levels, axis=0).astype(jnp.int32) - 32768
                code_ref[it, g, to * pairs + t] = level.astype(jnp.int16)
                return carry

            lax.fori_loop(0, pairs, encode, 0, unroll=True)
            copy = code_copy(it, g, d, to)
            copy.start()
            sent.append(copy)

    def update(it, g):
        for d in range(1, n_col):
            code_copy(it, g, d, c_to[d]).wait_recv()

        def one(t, carry):
            found = [
                code_in_ref[it, g, d, t].astype(jnp.int32).astype(jnp.float32) + 32768.0
                for d in range(1, n_col)
            ]
            values = []
            for i in range(2):
                b = 2 * t + i
                r = my_col * own + b
                prior = prior_ref[part(g), lanes(b)]
                total = prior if it == 0 else cur_ref[g, b]
                total = total + run_ref[g, plan_ref[2, r]] * plan_ref[3, r].astype(jnp.float32)
                for d in range(1, n_col):
                    level = found[d - 1][i * some : (i + 1) * some]
                    total = total + level * (rows_in_ref[d, pl.ds(b, 1), :] * (1.0 / LEVELS))
                value = total * scale_ref[pl.ds(b, 1), :] + (1.0 - SPREAD) * prior
                if it + 1 < ITERS:
                    cur_ref[g, b] = value
                    values.append(value)
                else:
                    out_ref[part(g), lanes(b)] = value
            if it + 1 < ITERS:
                ag_ref[it + 1, g, my_row * pairs + t] = jnp.concatenate(values, axis=0).astype(jnp.bfloat16)
            return carry

        lax.fori_loop(0, pairs, one, 0, unroll=True)

    for it in range(ITERS):
        for g in range(GROUPS):
            gather_finish(it, g, passed=it in LATE and g > 0)
            multiply(it, g)
            if it in LATE and g + 1 < GROUPS:
                for d in range(1, n_z):
                    gather_pass(it, g + 1, d)
            send_codes(it, g)
        if it == 0:
            degree = 1.0 + rows_ref[pl.ds(pl.multiple_of(my_col * own, own), own), :]
            for d in range(1, n_col):
                row_copy(d).wait_recv()
                degree = degree + rows_in_ref[d]
            scale_ref[...] = SPREAD / degree
        for g in range(GROUPS):
            update(it, g)
            if it + 1 < ITERS:
                gather_start(it + 1, g)

    for copy in sent:
        copy.wait_send()


def local(n_row, n_col, labels_prior, tiles, tile_rows, tile_cols, tile_count):
    labels, piece = labels_prior.shape
    slots, tile, _ = tiles.shape
    own = piece // tile
    pairs = own // 2
    some = labels // GROUPS
    n_z = n_row // 2
    group = n_col * own
    width = -(-max(slots, group) // 128) * 128
    vmem = pl.BlockSpec(memory_space=pltpu.VMEM)
    return pl.pallas_call(
        functools.partial(kernel, n_row, n_col),
        out_shape=pltpu.VMEM((labels, piece), jnp.float32),
        in_specs=[pl.BlockSpec(memory_space=pl.ANY)] * 5,
        out_specs=vmem,
        scratch_shapes=[
            pltpu.VMEM((labels, piece), jnp.float32),
            pltpu.VMEM((slots, tile, tile), jnp.bfloat16),
            pltpu.VMEM((ITERS, GROUPS, n_row * pairs, 2 * some, tile), jnp.bfloat16),
            pltpu.VMEM((n_row * own, 2 * some, tile), jnp.bfloat16),
            pltpu.VMEM((n_row * own, 2 * some, tile), jnp.bfloat16),
            pltpu.VMEM((GROUPS, slots, some, tile), jnp.float32),
            pltpu.VMEM((group, tile), jnp.float32),
            pltpu.VMEM((group, tile), jnp.float32),
            pltpu.VMEM((n_col, own, tile), jnp.float32),
            pltpu.VMEM((ITERS, GROUPS, n_col * pairs, 2 * some, tile), jnp.int16),
            pltpu.VMEM((ITERS, GROUPS, n_col, pairs, 2 * some, tile), jnp.int16),
            pltpu.VMEM((GROUPS, own, some, tile), jnp.float32),
            pltpu.VMEM((own, tile), jnp.float32),
            pltpu.VMEM((8, width), jnp.int32),
            pltpu.SMEM((8, width), jnp.int32),
            pltpu.VMEM((slots, tile), jnp.float32),
            pltpu.VMEM((slots, tile), jnp.float32),
            pltpu.VMEM((2, 1, slots), jnp.int32),
            pltpu.SMEM((1,), jnp.int32),
            pltpu.SemaphoreType.DMA((GROUPS,)),
            pltpu.SemaphoreType.DMA((LOADS,)),
            pltpu.SemaphoreType.DMA(()),
            pltpu.SemaphoreType.DMA((3,)),
            pltpu.SemaphoreType.DMA((ITERS, GROUPS, 2 * n_z)),
            pltpu.SemaphoreType.DMA((ITERS, GROUPS, 2 * n_z)),
            pltpu.SemaphoreType.DMA((ITERS, GROUPS, n_col)),
            pltpu.SemaphoreType.DMA((ITERS, GROUPS, n_col)),
            pltpu.SemaphoreType.DMA((n_col,)),
            pltpu.SemaphoreType.DMA((n_col,)),
        ],
        compiler_params=pltpu.CompilerParams(
            collective_id=0, has_side_effects=True, vmem_limit_bytes=56 * 1024 * 1024
        ),
    )(labels_prior, tiles, tile_rows.reshape(1, -1), tile_cols.reshape(1, -1), tile_count)


def solution(mesh):
    n_row, n_col = mesh.shape["row"], mesh.shape["col"]
    in_specs = (
        P(None, ("row", "col")),
        P(("row", "col"), None, None),
        P(("row", "col")),
        P(("row", "col")),
        P(("row", "col")),
    )
    return jax.shard_map(
        functools.partial(local, n_row, n_col),
        mesh=mesh,
        in_specs=in_specs,
        out_specs=P(None, ("row", "col")),
        check_vma=False,
    )
```

```python
import functools

import jax
import jax.numpy as jnp
from jax import lax
from jax.experimental import pallas as pl
from jax.experimental.pallas import tpu as pltpu
from jax.sharding import PartitionSpec as P

ITERS = 2
SPREAD = 0.9
LEVELS = 65535.0
GROUPS = 2
LOADS = 7
LATE = (ITERS - 1,)


def plan(rows, cols, count, table_ref, keep_ref, group_blocks):
    slots = rows.shape[1]
    lane = lax.broadcasted_iota(jnp.int32, (slots, slots), 1)
    down = lax.broadcasted_iota(jnp.int32, (slots, slots), 0)
    row = jnp.where(lane[0:1] < count, rows, group_blocks)
    key = row * slots + lane[0:1]
    same = lane == down

    def stand(x):
        return jnp.sum(jnp.where(same, x, 0), axis=1, keepdims=True)

    key_down, row_down, col_down = stand(key), stand(row), stand(cols)
    rank = jnp.sum((key < key_down).astype(jnp.int32), axis=1, keepdims=True)
    hit = rank == lane

    def lie(cond, x):
        return jnp.sum(jnp.where(cond, x, 0), axis=0, keepdims=True)

    here = lie(hit, row_down + 1)
    before = lie(rank + 1 == lane, row_down + 1)
    table_ref[0:1, 0:slots] = lie(hit, down)
    table_ref[1:2, 0:slots] = lie(hit, col_down)
    keep = stand((here == before).astype(jnp.int32)).astype(jnp.float32)
    keep_ref[...] = jnp.broadcast_to(keep, keep_ref.shape)
    group = lax.broadcasted_iota(jnp.int32, (slots, group_blocks), 1)
    stop = jnp.sum((row_down <= group).astype(jnp.int32), axis=0, keepdims=True)
    start = jnp.sum((row_down < group).astype(jnp.int32), axis=0, keepdims=True)
    table_ref[2:3, 0:group_blocks] = jnp.maximum(stop - 1, 0)
    table_ref[3:4, 0:group_blocks] = (stop > start).astype(jnp.int32)
    block = lax.broadcasted_iota(jnp.int32, (group_blocks, slots), 0)
    return (block == row).astype(jnp.float32)


def kernel(
    n_row, n_col,
    prior_hbm, tiles_hbm, slot_rows_hbm, slot_cols_hbm, count_hbm,
    out_ref,
    prior_ref, tiles_ref, ag_ref, upper_ref, lower_ref, run_ref, rows_ref, inv_ref, rows_in_ref, code_ref, code_in_ref,
    cur_ref, scale_ref, table_ref, plan_ref, keep_ref, slot_sum_ref, slots_ref, count_ref,
    prior_sem, load_sem, plan_sem, slots_sem, ag_send, ag_recv, rs_send, rs_recv, row_send, row_recv,
):
    labels, piece = prior_ref.shape
    slots, tile, _ = tiles_ref.shape
    own = piece // tile
    pairs = own // 2
    some = labels // GROUPS
    n_z = n_row // 2
    my_row = lax.axis_index("row")
    my_col = lax.axis_index("col")
    my_z = my_row // 2
    my_core = my_row % 2
    partner = my_z * 2 + (1 - my_core)

    def at(row, col):
        return {"row": row, "col": col}

    def part(g):
        return pl.ds(g * some, some)

    prior_copies = []
    for g in range(GROUPS):
        prior_copies.append(
            pltpu.make_async_copy(prior_hbm.at[part(g)], prior_ref.at[part(g)], prior_sem.at[g])
        )
        prior_copies[-1].start()

    barrier = pltpu.get_barrier_semaphore()
    z_to = [None] + [((my_z + d) % n_z) * 2 + my_core for d in range(1, n_z)]
    z_from = [None] + [((my_z + n_z - d) % n_z) * 2 + my_core for d in range(1, n_z)]
    asc = [None] + [(d - 1 + jnp.where(d - 1 < my_z, 0, 1)) * 2 + my_core for d in range(1, n_z)]
    p_from = [partner] + [((my_z + n_z - d) % n_z) * 2 + (1 - my_core) for d in range(1, n_z)]
    c_to = [None] + [(my_col + d) % n_col for d in range(1, n_col)]
    c_from = [None] + [(my_col + n_col - d) % n_col for d in range(1, n_col)]
    for d in range(1, n_z):
        pl.semaphore_signal(barrier, inc=1, device_id=at(z_to[d], my_col))
    pl.semaphore_signal(barrier, inc=1, device_id=at(partner, my_col))
    for d in range(1, n_col):
        pl.semaphore_signal(barrier, inc=1, device_id=at(my_row, c_to[d]))

    slot_copies = [
        pltpu.make_async_copy(slot_rows_hbm, slots_ref.at[0], slots_sem.at[0]),
        pltpu.make_async_copy(slot_cols_hbm, slots_ref.at[1], slots_sem.at[1]),
        pltpu.make_async_copy(count_hbm, count_ref, slots_sem.at[2]),
    ]
    for copy in slot_copies:
        copy.start()

    loads = []
    step = slots // LOADS
    for n in range(LOADS):
        window = pl.ds(n * step, step)
        loads.append(
            pltpu.make_async_copy(tiles_hbm.at[window], tiles_ref.at[window], load_sem.at[n])
        )
        loads[-1].start()

    sent = []

    def gather_copy(it, g, src_row, slot, to_row):
        window = pl.ds(src_row * pairs, pairs)
        return pltpu.make_async_remote_copy(
            src_ref=ag_ref.at[it, g, window],
            dst_ref=ag_ref.at[it, g, window],
            send_sem=ag_send.at[it, g, slot],
            recv_sem=ag_recv.at[it, g, (slot // n_z) * n_z + src_row // 2],
            device_id=at(to_row, my_col),
        )

    def expand(it, g, src_row):
        def one(t, carry):
            both = ag_ref[it, g, src_row * pairs + t].astype(jnp.float32)
            blank = jnp.zeros((some, tile), jnp.float32)
            b = src_row * own + 2 * t
            for i, half in enumerate((both[:some], both[some:])):
                upper_ref[b + i] = jnp.concatenate([half, blank], axis=0).astype(jnp.bfloat16)
                lower_ref[b + i] = jnp.concatenate([blank, half], axis=0).astype(jnp.bfloat16)
            return carry

        lax.fori_loop(0, pairs, one, 0, unroll=True)

    def gather_start(it, g):
        copies = [gather_copy(it, g, my_row, n_z, partner)]
        to = asc if it + 1 == ITERS else z_to
        copies += [gather_copy(it, g, my_row, d, to[d]) for d in range(1, n_z)]
        for copy in copies:
            copy.start()
        sent.extend(copies)

    def gather_pass(it, g, d):
        gather_copy(it, g, z_from[d], d, z_to[d]).wait_recv()
        copy = gather_copy(it, g, z_from[d], n_z + d, partner)
        copy.start()
        sent.append(copy)

    def gather_finish(it, g, passed=False):
        for d in range(1, n_z):
            if not passed:
                gather_pass(it, g, d)
        expand(it, g, my_row)
        for d in range(1, n_z):
            expand(it, g, z_from[d])
        for d in range(n_z):
            gather_copy(it, g, p_from[d], n_z + d, partner).wait_recv()
            expand(it, g, p_from[d])

    def lanes(b):
        return pl.ds(pl.multiple_of(b * tile, tile), tile)

    for g in range(GROUPS):

        def round_prior(t, carry):
            both = [prior_ref[part(g), lanes(2 * t + i)] for i in range(2)]
            ag_ref[0, g, my_row * pairs + t] = jnp.concatenate(both, axis=0).astype(jnp.bfloat16)
            return carry

        prior_copies[g].wait()
        lax.fori_loop(0, pairs, round_prior, 0, unroll=True)
        if g == 0:
            pl.semaphore_wait(barrier, n_z + n_col - 1)
        gather_start(0, g)

    def product(left, right):
        return lax.dot_general(
            left, right, (((1,), (0,)), ((), ())), preferred_element_type=jnp.float32
        )

    for copy in slot_copies:
        copy.wait()
    hot = plan(slots_ref[0], slots_ref[1], count_ref[0], table_ref, keep_ref, n_col * own)
    plan_copy = pltpu.make_async_copy(table_ref, plan_ref, plan_sem)
    plan_copy.start()

    def weights(slot_pair):
        return jnp.concatenate([tiles_ref[n] for n in slot_pair], axis=0)

    down = lax.broadcasted_iota(jnp.int32, (2 * some, 2 * tile), 0)
    lane = lax.broadcasted_iota(jnp.int32, (2 * some, 2 * tile), 1)
    ones = ((down < some) == (lane < tile)).astype(jnp.float32).astype(jnp.bfloat16)
    for n, copy in enumerate(loads):
        copy.wait()

        def sum_pair(m, carry):
            k = n * step + 2 * m
            for turned in (k, k + 1):
                tiles_ref[turned] = tiles_ref[turned].T
            both = product(ones, weights((k, k + 1)))
            for i in range(2):
                slot_sum_ref[pl.ds(k + i, 1), :] = both[i * some : i * some + 1]
            return carry

        lax.fori_loop(0, step // 2, sum_pair, 0, unroll=True)
    rows_ref[...] = jnp.dot(
        hot, slot_sum_ref[...], precision=lax.Precision.HIGHEST, preferred_element_type=jnp.float32
    )

    def row_copy(d):
        return pltpu.make_async_remote_copy(
            src_ref=rows_ref.at[pl.ds(pl.multiple_of(c_to[d] * own, own), own)],
            dst_ref=rows_in_ref.at[d],
            send_sem=row_send.at[d],
            recv_sem=row_recv.at[d],
            device_id=at(my_row, c_to[d]),
        )

    for d in range(1, n_col):
        copy = row_copy(d)
        copy.start()
        sent.append(copy)
    whole = rows_ref[...]
    inv_ref[...] = jnp.where(whole > 0.0, LEVELS / jnp.where(whole > 0.0, whole, 1.0), 0.0)
    plan_copy.wait()

    def code_copy(it, g, d, to):
        return pltpu.make_async_remote_copy(
            src_ref=code_ref.at[it, g, pl.ds(to * pairs, pairs)],
            dst_ref=code_in_ref.at[it, g, d],
            send_sem=rs_send.at[it, g, d],
            recv_sem=rs_recv.at[it, g, d],
            device_id=at(my_row, to),
        )

    def multiply(it, g):
        def add_pair(m, total):
            ks = (2 * m, 2 * m + 1)
            left = jnp.concatenate(
                [upper_ref[plan_ref[1, ks[0]]], lower_ref[plan_ref[1, ks[1]]]], axis=1
            )
            both = product(left, weights([plan_ref[0, k] for k in ks]))
            for i, k in enumerate(ks):
                keep = jnp.broadcast_to(keep_ref[pl.ds(k, 1), :], (some, tile))
                total = total * keep + both[i * some : (i + 1) * some]
                run_ref[g, k] = total
            return total

        lax.fori_loop(0, slots // 2, add_pair, jnp.zeros((some, tile), jnp.float32), unroll=True)

    def send_codes(it, g):
        for i in range(1, n_col):
            to = c_to[i]
            d = i
            if it + 1 == ITERS:
                to = i - 1 + jnp.where(i - 1 < my_col, 0, 1)
                d = (to + n_col - my_col) % n_col


            def encode(t, carry):
                levels = []
                for i in range(2):
                    r = to * own + 2 * t + i
                    value = run_ref[g, plan_ref[2, r]]
                    levels.append(jnp.minimum(value * inv_ref[pl.ds(r, 1), :] + 0.5, LEVELS))
                level = jnp.concatenate(levels, axis=0).astype(jnp.int32) - 32768
                code_ref[it, g, to * pairs + t] = level.astype(jnp.int16)
                return carry

            lax.fori_loop(0, pairs, encode, 0, unroll=True)
            copy = code_copy(it, g, d, to)
            copy.start()
            sent.append(copy)

    def update(it, g):
        for d in range(1, n_col):
            code_copy(it, g, d, c_to[d]).wait_recv()

        def one(t, carry):
            found = [
                code_in_ref[it, g, d, t].astype(jnp.int32).astype(jnp.float32) + 32768.0
                for d in range(1, n_col)
            ]
            values = []
            for i in range(2):
                b = 2 * t + i
                r = my_col * own + b
                prior = prior_ref[part(g), lanes(b)]
                total = prior if it == 0 else cur_ref[g, b]
                total = total + run_ref[g, plan_ref[2, r]] * plan_ref[3, r].astype(jnp.float32)
                for d in range(1, n_col):
                    level = found[d - 1][i * some : (i + 1) * some]
                    total = total + level * (rows_in_ref[d, pl.ds(b, 1), :] * (1.0 / LEVELS))
                value = total * scale_ref[pl.ds(b, 1), :] + (1.0 - SPREAD) * prior
                if it + 1 < ITERS:
                    cur_ref[g, b] = value
                    values.append(value)
                else:
                    out_ref[part(g), lanes(b)] = value
            if it + 1 < ITERS:
                ag_ref[it + 1, g, my_row * pairs + t] = jnp.concatenate(values, axis=0).astype(jnp.bfloat16)
            return carry

        lax.fori_loop(0, pairs, one, 0, unroll=True)

    for it in range(ITERS):
        for g in range(GROUPS):
            gather_finish(it, g, passed=it in LATE and g > 0)
            multiply(it, g)
            if it in LATE and g + 1 < GROUPS:
                for d in range(1, n_z):
                    gather_pass(it, g + 1, d)
            send_codes(it, g)
        if it == 0:
            degree = 1.0 + rows_ref[pl.ds(pl.multiple_of(my_col * own, own), own), :]
            for d in range(1, n_col):
                row_copy(d).wait_recv()
                degree = degree + rows_in_ref[d]
            scale_ref[...] = SPREAD / degree
        for g in range(GROUPS):
            update(it, g)
            if it + 1 < ITERS:
                gather_start(it + 1, g)

    for copy in sent:
        copy.wait_send()


def local(n_row, n_col, labels_prior, tiles, tile_rows, tile_cols, tile_count):
    labels, piece = labels_prior.shape
    slots, tile, _ = tiles.shape
    own = piece // tile
    pairs = own // 2
    some = labels // GROUPS
    n_z = n_row // 2
    group = n_col * own
    width = -(-max(slots, group) // 128) * 128
    vmem = pl.BlockSpec(memory_space=pltpu.VMEM)
    return pl.pallas_call(
        functools.partial(kernel, n_row, n_col),
        out_shape=pltpu.VMEM((labels, piece), jnp.float32),
        in_specs=[pl.BlockSpec(memory_space=pl.ANY)] * 5,
        out_specs=vmem,
        scratch_shapes=[
            pltpu.VMEM((labels, piece), jnp.float32),
            pltpu.VMEM((slots, tile, tile), jnp.bfloat16),
            pltpu.VMEM((ITERS, GROUPS, n_row * pairs, 2 * some, tile), jnp.bfloat16),
            pltpu.VMEM((n_row * own, 2 * some, tile), jnp.bfloat16),
            pltpu.VMEM((n_row * own, 2 * some, tile), jnp.bfloat16),
            pltpu.VMEM((GROUPS, slots, some, tile), jnp.float32),
            pltpu.VMEM((group, tile), jnp.float32),
            pltpu.VMEM((group, tile), jnp.float32),
            pltpu.VMEM((n_col, own, tile), jnp.float32),
            pltpu.VMEM((ITERS, GROUPS, n_col * pairs, 2 * some, tile), jnp.int16),
            pltpu.VMEM((ITERS, GROUPS, n_col, pairs, 2 * some, tile), jnp.int16),
            pltpu.VMEM((GROUPS, own, some, tile), jnp.float32),
            pltpu.VMEM((own, tile), jnp.float32),
            pltpu.VMEM((8, width), jnp.int32),
            pltpu.SMEM((8, width), jnp.int32),
            pltpu.VMEM((slots, tile), jnp.float32),
            pltpu.VMEM((slots, tile), jnp.float32),
            pltpu.VMEM((2, 1, slots), jnp.int32),
            pltpu.SMEM((1,), jnp.int32),
            pltpu.SemaphoreType.DMA((GROUPS,)),
            pltpu.SemaphoreType.DMA((LOADS,)),
            pltpu.SemaphoreType.DMA(()),
            pltpu.SemaphoreType.DMA((3,)),
            pltpu.SemaphoreType.DMA((ITERS, GROUPS, 2 * n_z)),
            pltpu.SemaphoreType.DMA((ITERS, GROUPS, 2 * n_z)),
            pltpu.SemaphoreType.DMA((ITERS, GROUPS, n_col)),
            pltpu.SemaphoreType.DMA((ITERS, GROUPS, n_col)),
            pltpu.SemaphoreType.DMA((n_col,)),
            pltpu.SemaphoreType.DMA((n_col,)),
        ],
        compiler_params=pltpu.CompilerParams(
            collective_id=0, has_side_effects=True, vmem_limit_bytes=56 * 1024 * 1024
        ),
    )(labels_prior, tiles, tile_rows.reshape(1, -1), tile_cols.reshape(1, -1), tile_count)


def solution(mesh):
    n_row, n_col = mesh.shape["row"], mesh.shape["col"]
    in_specs = (
        P(None, ("row", "col")),
        P(("row", "col"), None, None),
        P(("row", "col")),
        P(("row", "col")),
        P(("row", "col")),
    )
    return jax.shard_map(
        functools.partial(local, n_row, n_col),
        mesh=mesh,
        in_specs=in_specs,
        out_specs=P(None, ("row", "col")),
        check_vma=False,
    )
```
